256 devices in a mesh: leaf: 16 (over y, x), col: 16 (over z, core).
Axes of the slice: x: 4, y: 4, z: 8, core: 2. Of those that a mesh axis runs over, the one named last changes fastest.
Arguments:
- right_sides: bfloat16 [16, 2, 1792, 128], P('leaf', None, 'col'), may hold values from -6 to 6
- leaf_inverse: bfloat16 [16, 1792, 1792], P('leaf', 'col'), as said below
- upper_inverse: bfloat16 [16, 1792, 1792], P('leaf', 'col'), as said below
- leaf_update: bfloat16 [16, 4, 1792, 512], P('leaf', None, 'col'), may hold values from -0.0625 to 0.0625
- upper_update: bfloat16 [16, 4, 1792, 512], P('leaf', None, 'col'), may hold values from -0.0625 to 0.0625
- live_rows: int32 [16, 2], P('leaf'), may hold values from 896 to 1792, as said below
- tile_map: int32 [16, 2, 4, 512], P('leaf'), may hold values from 0 to 1791, as said below
Outputs:
- solution: bfloat16 [16, 2, 1792, 128], P('leaf', None, 'col')
The draws below stay inside these ranges and needn't reach their ends.
Inputs may be any that keep to these rules, and one draw needn't show every extreme that they name: `leaf_inverse`: zero above the diagonal, nonzero on it. `upper_inverse`: zero above the diagonal, nonzero on it. `live_rows`: one supernode has all 1792 rows live and one has 896. `tile_map`: the rows of one tile are distinct and increasing.
All inputs are finite; a program needn't handle non-finite values.
Results may differ from the reference program's by a relative error of at most 0.0075.
Values may be sent and summed in bfloat16 or wider, within the bound.
No kernel may reach another device: no remote copies, remote signals or barrier semaphores. Data moves between devices by JAX's collectives and lax.ppermute only.
A program may use at most 64 MiB of HBM per device.

```python
import jax
import jax.numpy as jnp
from jax import lax

SN = 1792
TILE = 512
ANC = 4
RHS = 128
N_LEAF = 16


def draw_triangle(key):
    first_key, second_key = jax.random.split(key)
    shape = (N_LEAF, SN, SN)
    row_ids = lax.broadcasted_iota(jnp.int32, (1, SN, SN), 1)
    col_ids = lax.broadcasted_iota(jnp.int32, (1, SN, SN), 2)
    diagonal = jax.random.uniform(first_key, (N_LEAF, SN, 1), jnp.float32, 0.6, 1.4)
    lower = jax.random.normal(second_key, shape, jnp.float32) * (0.5 / SN ** 0.5)
    zeros = jnp.zeros(shape, jnp.float32)
    result = jnp.where(row_ids == col_ids, diagonal, jnp.where(col_ids < row_ids, lower, zeros))
    return result.astype(jnp.bfloat16)


def draw_leaf_inverse(key, part):
    return draw_triangle(jax.random.fold_in(key, 11))


def draw_upper_inverse(key, part):
    return draw_triangle(jax.random.fold_in(key, 12))


def draw_live_rows(key, part):
    first_key, second_key, third_key = jax.random.split(jax.random.fold_in(key, 13), 3)
    total = N_LEAF * 2
    sizes = jax.random.randint(first_key, (total,), SN // 2, SN + 1, jnp.int32)
    place_full = jax.random.randint(second_key, (), 0, total, jnp.int32)
    place_half = (place_full + 1 + jax.random.randint(third_key, (), 0, total - 1, jnp.int32)) % total
    sizes = sizes.at[place_full].set(SN)
    sizes = sizes.at[place_half].set(SN // 2)
    return sizes.reshape(N_LEAF, 2)


def draw_tile_map(key, part):
    keys = jax.random.split(jax.random.fold_in(key, 14), N_LEAF * 2 * ANC)

    def one_tile(tile_key):
        return jnp.sort(jax.random.permutation(tile_key, SN)[:TILE]).astype(jnp.int32)
    return jax.vmap(one_tile)(keys).reshape(N_LEAF, 2, ANC, TILE)


def block_scale(rng, dims, cuts, least, high):
    def one(axis_at, shards_of):
        heights = jax.random.uniform(jax.random.fold_in(jax.random.fold_in(rng, 6), axis_at), (shards_of,), jnp.float32, least / len(cuts), high / len(cuts))
        return jnp.repeat(jnp.exp(heights), dims[axis_at] // shards_of).reshape((-1,) + (1,) * (len(dims) - axis_at - 1))

    loudness = one(*cuts[0])
    for cut in cuts[1:]:
        loudness = loudness * one(*cut)
    return loudness


def noise(own_key, shape, width, most, shards=(), kind=jnp.bfloat16):
    gain = block_scale(own_key, shape, shards, -0.22, 0.18) if shards else 1.0
    values = jax.random.normal(own_key, shape, jnp.float32) * width * gain
    return jnp.minimum(jnp.maximum(values, -most), most).astype(kind)


def setup_inputs(seed: int = 0) -> dict:
    key_list = jax.random.split(jax.random.key(seed), 8)
    return {
        "right_sides": noise(key_list[0], (N_LEAF, 2, SN, RHS), 1.0, 6.0, ((0, 16), (2, 16))),
        "leaf_inverse": draw_leaf_inverse(jax.random.fold_in(key_list[7], 71), 0),
        "upper_inverse": draw_upper_inverse(jax.random.fold_in(key_list[7], 71), 0),
        "leaf_update": noise(key_list[3], (N_LEAF, ANC, SN, TILE), (4 * SN) ** -0.5, 0.0625, ((0, 16), (2, 16))),
        "upper_update": noise(key_list[4], (N_LEAF, ANC, SN, TILE), (4 * SN) ** -0.5, 0.0625, ((0, 16), (2, 16))),
        "live_rows": draw_live_rows(jax.random.fold_in(key_list[7], 71), 0),
        "tile_map": draw_tile_map(jax.random.fold_in(key_list[7], 71), 0),
    }


def reference(right_sides, leaf_inverse, upper_inverse, leaf_update, upper_update, live_rows, tile_map):
    depth = N_LEAF.bit_length() - 1
    row_ids = jnp.arange(SN, dtype=jnp.int32)

    def row_mask(node, which):
        return (row_ids < live_rows[node, which]).astype(jnp.float32)[:, None]

    def level_of(node):
        return (node & -node).bit_length()

    def ancestor(node, height):
        return ((node >> height) << height) + (1 << (height - 1))

    def forward_solve(inverse, residual, masking):
        shares = (residual * masking).astype(jnp.bfloat16)
        return (jnp.dot(inverse, shares, preferred_element_type=jnp.float32) * masking).astype(jnp.bfloat16)

    def backward_solve(inverse, solved, pulled, masking):
        scaled = ((solved.astype(jnp.float32) - pulled) * masking).astype(jnp.bfloat16)
        return (jnp.dot(inverse.T, scaled, preferred_element_type=jnp.float32) * masking).astype(jnp.bfloat16)

    residual_up = {}
    for node in range(1, N_LEAF):
        residual_up[node] = right_sides[node, 1].astype(jnp.float32)

    def push(target, tile_rows, update, solved):
        residual_up[target] = residual_up[target].at[tile_rows].add(
            -jnp.dot(update.T, solved, preferred_element_type=jnp.float32))

    solved_leaf = {}
    for node in range(N_LEAF):
        solved = forward_solve(leaf_inverse[node], right_sides[node, 0].astype(jnp.float32), row_mask(node, 0))
        solved_leaf[node] = solved
        for slot_idx in range(depth):
            push(ancestor(node, slot_idx + 1), tile_map[node, 0, slot_idx], leaf_update[node, slot_idx], solved)

    solved_up = {}
    for height in range(1, depth + 1):
        for node in range(1, N_LEAF):
            if level_of(node) == height:
                solved = forward_solve(upper_inverse[node], residual_up[node], row_mask(node, 1))
                solved_up[node] = solved
                for slot_idx in range(depth - height):
                    push(ancestor(node, height + 1 + slot_idx), tile_map[node, 1, slot_idx], upper_update[node, slot_idx], solved)

    answer_up = {}
    for height in range(depth, 0, -1):
        for node in range(1, N_LEAF):
            if level_of(node) == height:
                pulled = jnp.zeros((SN, RHS), jnp.float32)
                for slot_idx in range(depth - height):
                    upper_x = answer_up[ancestor(node, height + 1 + slot_idx)]
                    picked = upper_x[tile_map[node, 1, slot_idx]]
                    pulled = pulled + jnp.dot(upper_update[node, slot_idx], picked, preferred_element_type=jnp.float32)
                answer_up[node] = backward_solve(upper_inverse[node], solved_up[node], pulled, row_mask(node, 1))

    blocks = []
    for node in range(N_LEAF):
        pulled = jnp.zeros((SN, RHS), jnp.float32)
        for slot_idx in range(depth):
            upper_x = answer_up[ancestor(node, slot_idx + 1)]
            picked = upper_x[tile_map[node, 0, slot_idx]]
            pulled = pulled + jnp.dot(leaf_update[node, slot_idx], picked, preferred_element_type=jnp.float32)
        answer_leaf = backward_solve(leaf_inverse[node], solved_leaf[node], pulled, row_mask(node, 0))
        if node == 0:
            answer_top = jnp.zeros((SN, RHS), jnp.bfloat16)
        else:
            answer_top = answer_up[node]
        blocks.append(jnp.stack([answer_leaf, answer_top]))
    return jnp.stack(blocks)
```

```python
import jax
import jax.numpy as jnp
from jax import lax
from jax.sharding import PartitionSpec as P

BF = jnp.bfloat16
F32 = jnp.float32


def dot(a, b, ca, cb):
    return lax.dot_general(a, b, (((ca,), (cb,)), ((), ())), preferred_element_type=F32)


def split_dot(a, b, ca, cb):
    hi = a.astype(BF)
    lo = (a - hi.astype(F32)).astype(BF)
    n = a.shape[0]
    both = dot(jnp.concatenate([hi, lo], axis=0), b, ca, cb)
    return both[:n] + both[n:]


def shards(
    right_sides, leaf_inverse, upper_inverse, leaf_update, upper_update, live_rows, tile_map
):
    leaf_count = lax.axis_size("leaf")
    col_count = lax.axis_size("col")
    depth = leaf_count.bit_length() - 1
    rows_dev = leaf_inverse.shape[1]
    rows = leaf_inverse.shape[2]
    width = right_sides.shape[3]
    part = width // col_count
    tile_len = tile_map.shape[3]
    leaf_id = lax.axis_index("leaf")
    col_id = lax.axis_index("col")

    all_rows = lax.broadcasted_iota(jnp.int32, (1, rows), 1)
    mask_up = (all_rows < live_rows[0, 1]).astype(F32)
    rows_full = lax.broadcasted_iota(jnp.int32, (rows, 1), 0)
    own_rows = col_id * rows_dev + lax.broadcasted_iota(jnp.int32, (rows_dev, 1), 0)
    mask_leaf = (own_rows < live_rows[0, 0]).astype(F32)

    node_level = jnp.zeros((), jnp.int32)
    for height in range(1, depth + 1):
        node_level = node_level + ((leaf_id % 2 ** (height - 1) == 0) & (leaf_id > 0)).astype(
            jnp.int32
        )

    inv_up = lax.all_gather(upper_inverse[0], "col", axis=0, tiled=True)
    upd_up = lax.all_gather(upper_update[0, : depth - 1], "col", axis=1, tiled=True)

    picks = (
        tile_map[0][:, :, :, None] == lax.broadcasted_iota(jnp.int32, (1, 1, 1, rows), 3)
    ).astype(BF)
    pick_leaf, pick_up = picks[0], picks[1]

    both = lax.all_gather(right_sides[0], "col", axis=1, tiled=True)
    r_leaf = jnp.where(rows_full < live_rows[0, 0], both[0], jnp.zeros_like(both[0]))
    base_up = lax.dynamic_slice_in_dim(both[1].T, col_id * part, part, 0).astype(F32)

    y_leaf = (dot(leaf_inverse[0], r_leaf, 1, 0) * mask_leaf).astype(BF)
    terms = jnp.concatenate(
        [dot(y_leaf, leaf_update[0, s], 0, 0) for s in range(depth)], axis=1
    ).astype(BF)
    swapped = lax.all_to_all(
        terms.reshape(col_count, part, depth * tile_len), "col", 0, 0, tiled=False
    )
    z_leaf = jnp.sum(swapped.astype(F32), axis=0)
    acc = jnp.stack(
        [
            split_dot(z_leaf[:, s * tile_len : (s + 1) * tile_len], pick_leaf[s], 1, 0)
            for s in range(depth)
        ]
    )

    nodes = range(1, leaf_count)

    def level_of(node):
        return (node & -node).bit_length()

    y_up = jnp.zeros((part, rows), BF)
    for height in range(1, depth + 1):
        if height == 1:
            got = lax.ppermute(acc, "leaf", [(i, i + 1) for i in range(0, leaf_count, 2)])
            acc = jnp.where(leaf_id % 2 == 1, acc + got, 0.0)
        else:
            step = 2 ** (height - 2)
            ups = [i for i in nodes if level_of(i) == height]
            acc = lax.ppermute(acc, "leaf", [(i - step, i) for i in ups]) + lax.ppermute(
                acc, "leaf", [(i + step, i) for i in ups]
            )
        r = ((base_up - acc[0]) * mask_up).astype(BF)
        y = (dot(r, inv_up, 1, 1) * mask_up).astype(BF)
        y_up = jnp.where(node_level == height, y, y_up)
        acc = acc[1:]
        if height < depth:
            acc = acc + jnp.stack(
                [
                    split_dot(dot(y, upd_up[s], 1, 0), pick_up[s], 1, 0)
                    for s in range(depth - height)
                ]
            )

    x_up = jnp.zeros((part, rows), BF)
    above = None
    for height in range(depth, 0, -1):
        if height == depth:
            pulled = jnp.zeros((part, rows), F32)
        else:
            pulled = sum(
                dot(dot(above[s], pick_up[s], 1, 1).astype(BF), upd_up[s], 1, 1)
                for s in range(depth - height)
            )
        v = ((y_up.astype(F32) - pulled) * mask_up).astype(BF)
        x = (dot(v, inv_up, 1, 0) * mask_up).astype(BF)
        x_up = jnp.where(node_level == height, x, x_up)
        above = x[None] if above is None else jnp.concatenate([x[None], above])
        if height == 1:
            got = lax.ppermute(above, "leaf", [(i + 1, i) for i in range(0, leaf_count, 2)])
            above = jnp.where(leaf_id % 2 == 1, above, got)
        else:
            step = 2 ** (height - 2)
            ups = [i for i in nodes if level_of(i) == height]
            above = lax.ppermute(above, "leaf", [(i, i - step) for i in ups]) + lax.ppermute(
                above, "leaf", [(i, i + step) for i in ups]
            )

    tiles = jnp.concatenate(
        [dot(above[s], pick_leaf[s], 1, 1).astype(BF) for s in range(depth)], axis=1
    )
    tiles = lax.all_gather(tiles, "col", axis=0, tiled=True)
    pulled = sum(
        dot(leaf_update[0, s], tiles[:, s * tile_len : (s + 1) * tile_len], 1, 1)
        for s in range(depth)
    )
    v = ((y_leaf.astype(F32) - pulled) * mask_leaf).astype(BF)
    terms = dot(leaf_inverse[0], v, 0, 0).astype(BF).reshape(col_count, rows_dev, width)
    swapped = lax.all_to_all(terms, "col", 0, 0, tiled=False)
    x_leaf = (jnp.sum(swapped.astype(F32), axis=0) * mask_leaf).astype(BF)

    x_up = jnp.where(leaf_id > 0, x_up, jnp.zeros_like(x_up))
    up_rows = lax.all_to_all(
        x_up.reshape(part, col_count, rows_dev).transpose(1, 0, 2), "col", 0, 0, tiled=False
    )
    up_rows = up_rows.reshape(width, rows_dev).T
    return jnp.stack([x_leaf, up_rows])[None]


def solution(mesh):
    placed = (
        P("leaf", None, "col", None),
        P("leaf", "col", None),
        P("leaf", "col", None),
        P("leaf", None, "col", None),
        P("leaf", None, "col", None),
        P("leaf", None),
        P("leaf", None, None, None),
    )
    return jax.shard_map(
        shards, mesh=mesh, in_specs=placed, out_specs=P("leaf", None, "col", None), check_vma=False
    )
```

```python
import functools

import jax
import jax.numpy as jnp
from jax import lax
from jax.experimental import pallas as pl
from jax.experimental.pallas import tpu as pltpu
from jax.sharding import PartitionSpec as P


BF = jnp.bfloat16
F32 = jnp.float32
VMEM_SPEC = pl.BlockSpec(memory_space=pltpu.VMEM)
SMEM_SPEC = pl.BlockSpec(memory_space=pltpu.SMEM)


def dot(a, b, ca, cb):
    return lax.dot_general(a, b, (((ca,), (cb,)), ((), ())), preferred_element_type=F32)


def call(body, outs, scalars, *args, scratch=()):
    return pl.pallas_call(
        body,
        out_shape=outs,
        in_specs=[SMEM_SPEC] + [VMEM_SPEC] * len(args),
        out_specs=jax.tree.map(lambda _: VMEM_SPEC, outs),
        scratch_shapes=list(scratch),
        compiler_params=pltpu.CompilerParams(vmem_limit_bytes=16 << 20),
    )(scalars, *args)


def row_mask(shape, live):
    return lax.broadcasted_iota(jnp.int32, shape, 1) < live


def one_pick(wanted, j):
    lanes = lax.broadcasted_iota(jnp.int32, wanted.shape, 1) + j * 128
    return jnp.where(wanted == lanes, 1.0, 0.0).astype(BF)


def picks_kernel(map_ref, pick_ref):
    slots, _, rows = pick_ref.shape


    @pl.loop(0, slots)
    def _(s):
        wanted = map_ref[s]
        for j in range(rows // 128):
            pick_ref[s, :, j * 128 : (j + 1) * 128] = one_pick(wanted, j)


def make_picks(wide, rows):
    slots, tile_len, _ = wide.shape
    return pl.pallas_call(
        picks_kernel,
        out_shape=jax.ShapeDtypeStruct((slots, tile_len, rows), BF),
        in_specs=[VMEM_SPEC],
        out_specs=VMEM_SPEC,
        compiler_params=pltpu.CompilerParams(vmem_limit_bytes=16 << 20),
        name="make_picks",
    )(wide)


def leaf_up_kernel(sc_ref, parts_ref, map_ref, acc_ref, base_ref, z_ref):
    slots, tile_len, _ = map_ref.shape
    groups, _ = parts_ref.shape[:2]
    rows = base_ref.shape[1]
    rows_dev, size = rows // (2 * groups), slots * tile_len
    total = parts_ref[0, :, :size].astype(F32)
    for k in range(1, groups):
        total = total + parts_ref[k, :, :size].astype(F32)
    for s in range(slots):
        z_ref[s] = total[:, s * tile_len : (s + 1) * tile_len]

    @pl.loop(0, slots)
    def _(s):
        z = z_ref[s].astype(BF)
        wanted = map_ref[s]
        for j in range(rows // 256):
            pick = jnp.concatenate([one_pick(wanted, 2 * j), one_pick(wanted, 2 * j + 1)], axis=1)
            acc_ref[s, :, j * 256 : (j + 1) * 256] = dot(z, pick, 1, 0).astype(BF)

    pieces = []
    for g in range(groups):
        for p in range(2):
            pieces.append(parts_ref[g, :, size + 128 * p : size + 128 * (p + 1)].astype(F32)[:, :rows_dev])
    base_ref[...] = jnp.concatenate(pieces, axis=1).astype(BF)


def up_kernel(height, sc_ref, base_ref, acc_a, acc_b, y_old, inv_ref, upd_ref, pick_ref, *outs):
    y_ref = outs[0]
    mask = row_mask(base_ref.shape, sc_ref[1])
    left = base_ref[...].astype(F32) - (acc_a[0].astype(F32) + acc_b[0].astype(F32))
    r = jnp.where(mask, left, 0.0).astype(BF)
    half = r.shape[1] // 2
    y = jnp.concatenate(
        [dot(r[:, :half], inv_ref[:half, :half], 1, 1), dot(r, inv_ref[half:, :], 1, 1)], axis=1
    )
    y = jnp.where(mask, y, 0.0).astype(BF)
    y_ref[...] = jnp.where(sc_ref[2] == height, y, y_old[...])
    if len(outs) > 1:
        acc_ref = outs[1]


        @pl.loop(0, acc_ref.shape[0])
        def _(s):
            z = dot(y, upd_ref[s], 1, 0).astype(BF)
            moved = dot(z, pick_ref[s], 1, 0)
            acc_ref[s] = (acc_a[s + 1].astype(F32) + acc_b[s + 1].astype(F32) + moved).astype(BF)


def down_kernel(height, sc_ref, y_ref, abo_a, abo_b, x_old, inv_ref, upd_ref, pick_ref, x_ref, out_ref):
    slots = out_ref.shape[0] - 1
    mask = row_mask(y_ref.shape, sc_ref[1])

    def pull(s, left):
        above = abo_a[s] + abo_b[s]
        out_ref[s + 1] = above
        tile = dot(above, pick_ref[s], 1, 1).astype(BF)
        return left - dot(tile, upd_ref[s], 1, 1)

    left = lax.fori_loop(0, slots, pull, y_ref[...].astype(F32))
    v = jnp.where(mask, left, 0.0).astype(BF)
    half = v.shape[1] // 2
    x = jnp.concatenate(
        [dot(v, inv_ref[:, :half], 1, 0), dot(v[:, half:], inv_ref[half:, half:], 1, 0)], axis=1
    )
    x = jnp.where(mask, x, 0.0).astype(BF)
    out_ref[0] = x
    x_ref[...] = jnp.where(sc_ref[2] == height, x, x_old[...])


def tiles_kernel(sc_ref, above_ref, pick_ref, tile_ref):
    slots, tile_len, _ = pick_ref.shape


    @pl.loop(0, slots)
    def _(s):
        here = pl.ds(pl.multiple_of(s * tile_len, 128), tile_len)
        tile_ref[:, here] = dot(above_ref[s], pick_ref[s], 1, 1).astype(BF)


def own_tiles_kernel(sc_ref, above_ref, map_ref, tile_ref):
    slots, tile_len, _ = map_ref.shape
    rows = above_ref.shape[2]

    @pl.loop(0, slots)
    def _(s):
        here = pl.ds(pl.multiple_of(s * tile_len, 128), tile_len)
        wanted = map_ref[s]
        above = above_ref[s]
        total = jnp.zeros((above.shape[0], tile_len), F32)
        for j in range(rows // 256):
            pick = jnp.concatenate([one_pick(wanted, 2 * j), one_pick(wanted, 2 * j + 1)], axis=1)
            total = total + dot(above[:, j * 256 : (j + 1) * 256], pick, 1, 1)
        tile_ref[:, here] = total.astype(BF)


def pack_kernel(sc_ref, inv_ref, upd_ref, fold_ref, half_ref, out_ref):
    col = sc_ref[4]
    low = out_ref.shape[1] - upd_ref.shape[0] * upd_ref.shape[2]
    tiles, spare = low // 128, fold_ref.shape[1] // 128
    for k in range(tiles):
        mine = inv_ref[:, k * 128 : (k + 1) * 128]
        m = tiles - 1 - k
        if m < spare:
            other = fold_ref[:, m * 128 : (m + 1) * 128]
        else:
            other = jnp.zeros_like(mine)
        own = jnp.where((col >= tiles) | (col >= k), 1, 0)
        keep = jnp.full(mine.shape, own, jnp.int32) == 1
        tile = jnp.where(keep, mine.astype(F32), other.astype(F32)).astype(BF)
        half_ref[:, k * 128 : (k + 1) * 128] = tile
        out_ref[:, k * 128 : (k + 1) * 128] = tile
    for s in range(upd_ref.shape[0]):
        size = upd_ref.shape[2]
        out_ref[:, low + s * size : low + (s + 1) * size] = upd_ref[s]


def join_kernel(sc_ref, upd_a, half_a, upd_b, half_b, out_a, out_b):
    for upd_ref, half_ref, out_ref in ((upd_a, half_a, out_a), (upd_b, half_b, out_b)):
        low, size = half_ref.shape[1], upd_ref.shape[2]
        out_ref[:, :low] = half_ref[...]
        for s in range(upd_ref.shape[0]):
            out_ref[:, low + s * size : low + (s + 1) * size] = upd_ref[s]


def place(col, first, chunk, inv_ref, upd_ref, blocks):
    count, rows_dev = chunk.shape[0], inv_ref.shape[0] // blocks
    low = chunk.shape[1] - upd_ref.shape[0] * upd_ref.shape[2]
    tiles, spare = low // 128, (inv_ref.shape[1] - low) // 128
    base = col * rows_dev + first
    other = (blocks - 1 - col) * rows_dev + first

    @pl.loop(0, count // 16)
    def _(i):
        at = pl.ds(pl.multiple_of(i * 16, 16), 16)
        here = pl.ds(pl.multiple_of(base + i * 16, 16), 16)
        there = pl.ds(pl.multiple_of(other + i * 16, 16), 16)
        for s in range(upd_ref.shape[0]):
            size = upd_ref.shape[2]
            upd_ref[s, here, :] = chunk[at, low + s * size : low + (s + 1) * size]

        @pl.when(col >= tiles)
        def _():
            inv_ref[here, :low] = chunk[at, :low]

        @pl.when(col < tiles)
        def _():
            for k in range(tiles):
                tile = chunk[at, k * 128 : (k + 1) * 128].astype(F32)
                own = jnp.full(tile.shape, jnp.where(col >= k, 1, 0), jnp.int32) == 1
                inv_ref[here, k * 128 : (k + 1) * 128] = jnp.where(own, tile, 0.0).astype(BF)
                m = tiles - 1 - k
                if m < spare:
                    to = low + m * 128
                    inv_ref[there, to : to + 128] = jnp.where(own, 0.0, tile).astype(BF)
            inv_ref[here, low:] = jnp.zeros((16, spare * 128), BF)


def gather_kernel(blocks, origins, firsts, sc_ref, *refs):
    chunks, (inv_ref, upd_ref) = refs[: len(origins)], refs[-2:]
    for chunk, (shift, flip), first in zip(chunks, origins, firsts):
        col = lax.rem(sc_ref[4] + 2 * shift + blocks, blocks)
        if flip:
            col = col + 1 - 2 * lax.rem(col, 2)
        place(col, first, chunk, inv_ref, upd_ref, blocks)


def leaf_fwd_kernel(sc_ref, r_ref, base_ref, inv_ref, upd_ref, y_ref, keep_ref, send_ref):
    rows_dev = inv_ref.shape[0]
    groups, part, _ = keep_ref.shape
    live_r = lax.broadcasted_iota(jnp.int32, r_ref.shape, 0) < sc_ref[0]
    r = jnp.where(live_r, r_ref[...].astype(F32), 0.0).astype(BF)
    mask = lax.broadcasted_iota(jnp.int32, y_ref.shape, 0) + sc_ref[4] * rows_dev < sc_ref[0]
    y = jnp.where(mask, dot(inv_ref[...], r, 1, 0), 0.0)
    y_ref[...] = y.astype(BF)
    turned = y.T.astype(BF)
    core = lax.rem(sc_ref[4], 2)
    slots, size = upd_ref.shape[0], upd_ref.shape[2]
    first = jnp.full((part, size), core, jnp.int32) == 0
    for s in range(slots):
        term = dot(turned, upd_ref[s], 1, 0)
        for g in range(groups):
            a = term[2 * g * part : (2 * g + 1) * part]
            b = term[(2 * g + 1) * part : (2 * g + 2) * part]
            keep_ref[g, :, s * size : (s + 1) * size] = jnp.where(first, a, b).astype(BF)
            send_ref[g, :, s * size : (s + 1) * size] = jnp.where(first, b, a).astype(BF)
    base = base_ref[...].astype(F32)
    base = jnp.concatenate([base, jnp.zeros((128 - rows_dev, base.shape[1]), F32)], axis=0).T
    first = jnp.full((part, 128), core, jnp.int32) == 0
    for g in range(groups):
        a = base[2 * g * part : (2 * g + 1) * part]
        b = base[(2 * g + 1) * part : (2 * g + 2) * part]
        keep_ref[g, :, slots * size :] = jnp.where(first, a, b).astype(BF)
        send_ref[g, :, slots * size :] = jnp.where(first, b, a).astype(BF)


def join_terms_kernel(sc_ref, keep_ref, got_ref, out_ref):
    groups, part, wide = keep_ref.shape
    size = wide - 128
    first = jnp.full((part, 128), lax.rem(sc_ref[4], 2), jnp.int32) == 0
    for g in range(groups):
        both = keep_ref[g, :, :size].astype(F32) + got_ref[g, :, :size].astype(F32)
        out_ref[g, :, :size] = both.astype(BF)
        own, other = keep_ref[g, :, size:].astype(F32), got_ref[g, :, size:].astype(F32)
        out_ref[g, :, size : size + 128] = jnp.where(first, own, other).astype(BF)
        out_ref[g, :, size + 128 :] = jnp.where(first, other, own).astype(BF)


def leaf_bwd_kernel(sc_ref, tile_ref, y_ref, upd_ref, inv_ref, x_ref, keep_ref, send_ref):
    rows_dev, width = y_ref.shape
    groups, part = keep_ref.shape[0], x_ref.shape[0]
    slots, size = upd_ref.shape[0], upd_ref.shape[2]
    left = y_ref[...].astype(F32)
    for s in range(slots):
        left = left - dot(upd_ref[s], tile_ref[:, s * size : (s + 1) * size], 1, 1)
    mask = lax.broadcasted_iota(jnp.int32, left.shape, 0) + sc_ref[4] * rows_dev < sc_ref[0]
    v = jnp.where(mask, left, 0.0).astype(BF)
    term = dot(inv_ref[...], v, 0, 0)
    core = lax.rem(sc_ref[4], 2)
    first = jnp.full((rows_dev, width), core, jnp.int32) == 0
    first_x = jnp.full((16, 128), core, jnp.int32) == 0
    x = x_ref[...].astype(F32)

    def block(at):
        piece = x[:, at * rows_dev : (at + 1) * rows_dev]
        piece = jnp.concatenate([piece, jnp.zeros((part, 128 - rows_dev), F32)], axis=1)
        return jnp.concatenate([piece, jnp.zeros((16 - part, 128), F32)], axis=0)

    for g in range(groups):
        a = term[2 * g * rows_dev : (2 * g + 1) * rows_dev]
        b = term[(2 * g + 1) * rows_dev : (2 * g + 2) * rows_dev]
        keep_ref[g, :rows_dev] = jnp.where(first, a, b).astype(BF)
        send_ref[g, :rows_dev] = jnp.where(first, b, a).astype(BF)
        xa, xb = block(2 * g), block(2 * g + 1)
        keep_ref[g, rows_dev:] = jnp.where(first_x, xa, xb).astype(BF)
        send_ref[g, rows_dev:] = jnp.where(first_x, xb, xa).astype(BF)


def merge_kernel(sc_ref, keep_ref, got_ref, out_ref):
    rows_dev = keep_ref.shape[1] - 16
    first = jnp.full((16, 128), lax.rem(sc_ref[4], 2), jnp.int32) == 0
    for g in range(keep_ref.shape[0]):
        both = keep_ref[g, :rows_dev].astype(F32) + got_ref[g, :rows_dev].astype(F32)
        out_ref[g, :rows_dev] = both.astype(BF)
        own, other = keep_ref[g, rows_dev:].astype(F32), got_ref[g, rows_dev:].astype(F32)
        out_ref[g, rows_dev : rows_dev + 16] = jnp.where(first, own, other).astype(BF)
        out_ref[g, rows_dev + 16 :] = jnp.where(first, other, own).astype(BF)


def final_kernel(sc_ref, in_ref, out_ref, wide_ref):
    rows_dev = out_ref.shape[1]
    groups, part = in_ref.shape[0], out_ref.shape[2] // (2 * in_ref.shape[0])
    total = in_ref[0, :rows_dev].astype(F32)
    for g in range(1, groups):
        total = total + in_ref[g, :rows_dev].astype(F32)
    mask = lax.broadcasted_iota(jnp.int32, total.shape, 0) + sc_ref[4] * rows_dev < sc_ref[0]
    out_ref[0] = jnp.where(mask, total, 0.0).astype(BF)
    for g in range(groups):
        for p in range(2):
            at, to = rows_dev + 16 * p, (2 * g + p) * part
            wide_ref[to : to + part] = in_ref[g, at : at + 16].astype(F32)[:part]
    out_ref[1] = wide_ref[...].T[:rows_dev].astype(BF)


def shards(
    right_sides, leaf_inverse, upper_inverse, leaf_update, upper_update, live_rows, tile_map
):
    leaf_count = lax.axis_size("leaf")
    col_count = lax.axis_size("col")
    depth = leaf_count.bit_length() - 1
    rows_dev = leaf_inverse.shape[1]
    rows = leaf_inverse.shape[2]
    width = right_sides.shape[3]
    part = width // col_count
    tile_len = tile_map.shape[3]
    leaf_id = lax.axis_index("leaf")
    col_id = lax.axis_index("col")

    node_level = jnp.zeros((), jnp.int32)
    for height in range(1, depth + 1):
        node_level = node_level + ((leaf_id % 2 ** (height - 1) == 0) & (leaf_id > 0)).astype(
            jnp.int32
        )
    scalars = jnp.stack([live_rows[0, 0], live_rows[0, 1], node_level, leaf_id % 2, col_id])

    wide_map = jnp.broadcast_to(tile_map[0, :, :, :, None], (2, depth, tile_len, 128))
    shape = jax.ShapeDtypeStruct
    blocks = col_count
    groups = blocks // 2
    low = rows // 2 + 128
    pairs = [(i, i ^ 1) for i in range(blocks)]
    members = [list(range(p, blocks, 2)) for p in range(2)]

    def along(x, step):
        return lax.ppermute(x, "col", [(i, (i + 2 * step) % blocks) for i in range(blocks)])

    def partner(x):
        return lax.ppermute(x, "col", pairs)

    own_upd = upper_update[0, : depth - 1]
    fold = lax.ppermute(
        upper_inverse[0, :, low:], "col", [(i, blocks - 1 - i) for i in range(blocks // 2, blocks)]
    )
    upd_a, upd_b = along(own_upd, 1), along(own_upd, -1)
    r_leaf = lax.all_gather(right_sides[0, 0], "col", axis=0, tiled=True)
    next_map = lax.ppermute(tile_map[0, 0], "leaf", [(i, i + 1) for i in range(0, leaf_count, 2)])
    fold, r_leaf, next_map = lax.optimization_barrier((fold, r_leaf, next_map))
    wide_next = jnp.broadcast_to(next_map[:, :, None], (depth, tile_len, 128))
    half, pack = call(
        pack_kernel,
        [shape((rows_dev, low), BF), shape((rows_dev, low + (depth - 1) * tile_len), BF)],
        scalars,
        upper_inverse[0],
        own_upd,
        fold,
    )
    half_a, half_b = along(half, 1), along(half, -1)
    y_leaf, keep, send = call(
        leaf_fwd_kernel,
        [shape((rows_dev, width), BF)] + [shape((groups, part, depth * tile_len + 128), BF)] * 2,
        scalars,
        r_leaf,
        right_sides[0, 1],
        leaf_inverse[0],
        leaf_update[0],
    )
    terms = call(
        join_terms_kernel,
        shape((groups, part, depth * tile_len + 256), BF),
        scalars,
        keep,
        partner(send),
    )
    swapped = lax.all_to_all(terms, "col", 0, 0, axis_index_groups=members)
    half_a, half_b, terms = lax.optimization_barrier((half_a, half_b, terms))
    ahead, behind = call(
        join_kernel, [shape(pack.shape, BF)] * 2, scalars, upd_a, half_a, upd_b, half_b
    )
    cut = rows_dev // 32 * 16 + 16
    chunks, origins, firsts = [pack, partner(pack)], [(0, False), (0, True)], [0, 0]
    for hop in range(1, groups // 2):
        if hop > 1:
            ahead, behind = along(ahead, 1), along(behind, -1)
        chunks += [ahead, behind, partner(ahead), partner(behind)]
        origins += [(-hop, False), (hop, False), (-hop, True), (hop, True)]
        firsts += [0] * 4
    acc, base_up = call(
        leaf_up_kernel,
        [shape((depth, part, rows), BF), shape((part, rows), BF)],
        scalars,
        swapped,
        wide_map[0],
        scratch=[pltpu.VMEM((depth, part, tile_len), F32)],
    )
    from_leaf = lax.ppermute(acc, "leaf", [(i, i + 1) for i in range(0, leaf_count, 2)])
    ahead, behind, acc = lax.optimization_barrier((ahead, behind, acc))
    far = groups // 2
    top, bottom = along(ahead[:cut], 1), along(behind[cut:], -1)
    last = [top, bottom, partner(top), partner(bottom)]
    last_origins = [(-far, False), (far, False), (-far, True), (far, True)]
    last_firsts = [0, cut, 0, cut]
    gathered = [shape((rows, rows), BF), shape((depth - 1, rows, tile_len), BF)]
    inv_up, upd_up = call(
        functools.partial(gather_kernel, blocks, origins, firsts), gathered, scalars, *chunks
    )
    inv_up, upd_up = pl.pallas_call(
        functools.partial(gather_kernel, blocks, last_origins, last_firsts),
        out_shape=gathered,
        in_specs=[SMEM_SPEC] + [VMEM_SPEC] * 6,
        out_specs=[VMEM_SPEC] * 2,
        input_output_aliases={5: 0, 6: 1},
        compiler_params=pltpu.CompilerParams(vmem_limit_bytes=16 << 20),
        name="gather_far",
    )(scalars, *last, inv_up, upd_up)

    pick_up = make_picks(wide_map[1, : depth - 1], rows)

    nodes = range(1, leaf_count)

    def level_of(node):
        return (node & -node).bit_length()

    y_up = jnp.zeros((part, rows), BF)
    for height in range(1, depth + 1):
        if height == 1:
            acc_a = acc
            acc_b = from_leaf
        else:
            step = 2 ** (height - 2)
            ups = [i for i in nodes if level_of(i) == height]
            acc_a = lax.ppermute(acc, "leaf", [(i - step, i) for i in ups])
            acc_b = lax.ppermute(acc, "leaf", [(i + step, i) for i in ups])
        if height == 2:
            acc_a, acc_b, next_pick = lax.optimization_barrier((acc_a, acc_b, next_pick))
        outs = [shape((part, rows), BF)]
        if height < depth:
            outs.append(shape((depth - height, part, rows), BF))
        y_up, *rest = call(
            functools.partial(up_kernel, height),
            outs,
            scalars,
            base_up,
            acc_a,
            acc_b,
            y_up,
            inv_up,
            upd_up,
            pick_up,
        )
        if rest:
            acc = rest[0]
        if height == 1:
            acc, wide_next = lax.optimization_barrier((acc, wide_next))
            next_pick = make_picks(wide_next, rows)

    x_up = jnp.zeros((part, rows), BF)
    abo_a = abo_b = jnp.zeros((1, part, rows), BF)
    for height in range(depth, 0, -1):
        x_up, above = call(
            functools.partial(down_kernel, height),
            [shape((part, rows), BF), shape((depth - height + 1, part, rows), BF)],
            scalars,
            y_up,
            abo_a,
            abo_b,
            x_up,
            inv_up,
            upd_up,
            pick_up,
        )
        if height == 1:
            sent = call(
                tiles_kernel, shape((part, depth * tile_len), BF), scalars, above, next_pick
            )
            got = lax.ppermute(sent, "leaf", [(i + 1, i) for i in range(0, leaf_count, 2)])
        else:
            step = 2 ** (height - 2)
            ups = [i for i in nodes if level_of(i) == height]
            abo_a = lax.ppermute(above, "leaf", [(i, i - step) for i in ups])
            abo_b = lax.ppermute(above, "leaf", [(i, i + step) for i in ups])

    tiles = call(own_tiles_kernel, shape((part, depth * tile_len), BF), scalars, above, wide_map[0])
    tiles = jnp.where(leaf_id % 2 == 1, tiles, got)
    tiles = lax.all_gather(tiles, "col", axis=0, tiled=True)
    keep, send = call(
        leaf_bwd_kernel,
        [shape((groups, rows_dev + 16, width), BF)] * 2,
        scalars,
        tiles,
        y_leaf,
        leaf_update[0],
        leaf_inverse[0],
        x_up,
    )
    merged = call(
        merge_kernel, shape((groups, rows_dev + 32, width), BF), scalars, keep, partner(send)
    )
    swapped = lax.all_to_all(merged, "col", 0, 0, axis_index_groups=members)
    return call(
        final_kernel,
        shape((2, rows_dev, width), BF),
        scalars,
        swapped,
        scratch=[pltpu.VMEM((width, 128), F32)],
    )[None]


def solution(mesh):
    placed = (
        P("leaf", None, "col", None),
        P("leaf", "col", None),
        P("leaf", "col", None),
        P("leaf", None, "col", None),
        P("leaf", None, "col", None),
        P("leaf", None),
        P("leaf", None, None, None),
    )

    return jax.shard_map(
        shards, mesh=mesh, in_specs=placed, out_specs=P("leaf", None, "col", None), check_vma=False
    )
```

```python
import functools

import jax
import jax.numpy as jnp
from jax import lax
from jax.experimental import pallas as pl
from jax.experimental.pallas import tpu as pltpu
from jax.sharding import PartitionSpec as P


BF = jnp.bfloat16
F32 = jnp.float32
PREP_LIMIT = 61
VMEM_SPEC = pl.BlockSpec(memory_space=pltpu.VMEM)
SMEM_SPEC = pl.BlockSpec(memory_space=pltpu.SMEM)


def dot(a, b, ca, cb):
    return lax.dot_general(a, b, (((ca,), (cb,)), ((), ())), preferred_element_type=F32)


def call(body, outs, live, *args, scratch=(), specs=None, limit=10):
    return pl.pallas_call(
        body,
        out_shape=outs,
        in_specs=[SMEM_SPEC] + [spec or VMEM_SPEC for spec in (specs or [None] * len(args))],
        out_specs=jax.tree.map(lambda _: VMEM_SPEC, outs),
        scratch_shapes=list(scratch),
        compiler_params=pltpu.CompilerParams(vmem_limit_bytes=limit << 20),
    )(live, *args)


def live_leaf(sc_ref):
    return sc_ref[0, 0]


def live_up(sc_ref):
    return sc_ref[0, 1]


def col_id():
    return lax.axis_index("col")


def node_level():
    leaf = lax.axis_index("leaf")
    level = jnp.where(leaf > 0, 1, 0)
    for height in range(1, lax.axis_size("leaf").bit_length() - 1):
        level = level + jnp.where((leaf > 0) & (lax.rem(leaf, 2**height) == 0), 1, 0)
    return level


def row_mask(shape, live):
    return lax.broadcasted_iota(jnp.int32, shape, 1) < live


def one_pick(wanted, j):
    lanes = lax.broadcasted_iota(jnp.int32, wanted.shape, 1) + j * 128
    return jnp.where(wanted == lanes, 1.0, 0.0).astype(BF)


def picks_kernel(map_ref, pick_ref):
    slots, _, rows = pick_ref.shape


    @pl.loop(0, slots)
    def _(s):
        wanted = map_ref[s]

        @pl.loop(0, rows // 128)
        def _(j):
            pick_ref[s, :, pl.ds(pl.multiple_of(j * 128, 128), 128)] = one_pick(wanted, j)


def make_picks(wide, rows):
    slots, tile_len, _ = wide.shape
    return pl.pallas_call(
        picks_kernel,
        out_shape=jax.ShapeDtypeStruct((slots, tile_len, rows), BF),
        in_specs=[VMEM_SPEC],
        out_specs=VMEM_SPEC,
        compiler_params=pltpu.CompilerParams(vmem_limit_bytes=10 << 20),
        name="make_picks",
    )(wide)


def leaf_up_kernel(sc_ref, parts_ref, map_ref, rows_ref, acc_ref, base_ref, z_ref):
    slots, tile_len, _ = map_ref.shape
    groups, part = parts_ref.shape[:2]
    rows = base_ref.shape[1]
    rows_dev, size = rows // (2 * groups), slots * tile_len
    total = parts_ref[0, :, :size].astype(F32)
    for k in range(1, groups):
        total = total + parts_ref[k, :, :size].astype(F32)
    for s in range(slots):
        z_ref[s] = total[:, s * tile_len : (s + 1) * tile_len]

    @pl.loop(0, slots)
    def _(s):
        z = z_ref[s].astype(BF)
        wanted = map_ref[s]

        for j in range(rows // 256):
            pick = jnp.concatenate([one_pick(wanted, 2 * j), one_pick(wanted, 2 * j + 1)], axis=1)
            acc_ref[s, :, j * 256 : (j + 1) * 256] = dot(z, pick, 1, 0).astype(BF)

    pieces = []
    for g in range(groups):
        for p in range(2):
            pieces.append(parts_ref[g, :, size + 128 * p : size + 128 * (p + 1)].astype(F32)[:, :rows_dev])
    base_ref[...] = jnp.concatenate(pieces, axis=1).astype(BF)
    high = (rows_ref[...] >> 7).astype(F32)
    low = (rows_ref[...] & 127).astype(F32)
    acc_ref[slots] = jnp.zeros((part, rows), BF)
    acc_ref[slots, :, :tile_len] = jnp.concatenate([high, low], axis=0).astype(BF)


def up_kernel(height, sc_ref, base_ref, acc_a, acc_b, y_old, inv_ref, upd_ref, pick_ref, *outs):
    y_ref = outs[0]
    mask = row_mask(base_ref.shape, live_up(sc_ref))
    left = base_ref[...].astype(F32) - (acc_a[0].astype(F32) + acc_b[0].astype(F32))
    r = jnp.where(mask, left, 0.0).astype(BF)
    half = r.shape[1] // 2
    y = jnp.concatenate(
        [dot(r[:, :half], inv_ref[:half, :half], 1, 1), dot(r, inv_ref[half:, :], 1, 1)], axis=1
    )
    y = jnp.where(mask, y, 0.0).astype(BF)
    y_ref[...] = jnp.where(node_level() == height, y, y_old[...])
    if len(outs) > 1:
        acc_ref = outs[1]


        @pl.loop(0, acc_ref.shape[0])
        def _(s):
            z = dot(y, upd_ref[s], 1, 0).astype(BF)
            moved = dot(z, pick_ref[s], 1, 0)
            acc_ref[s] = (acc_a[s + 1].astype(F32) + acc_b[s + 1].astype(F32) + moved).astype(BF)


def down_kernel(height, sc_ref, y_ref, abo_a, abo_b, x_old, inv_ref, upd_ref, pick_ref, x_ref, out_ref):
    slots = out_ref.shape[0] - 1
    mask = row_mask(y_ref.shape, live_up(sc_ref))

    def pull(s, left):
        above = abo_a[s] + abo_b[s]
        out_ref[s + 1] = above
        tile = dot(above, pick_ref[s], 1, 1).astype(BF)
        return left - dot(tile, upd_ref[s], 1, 1)

    left = lax.fori_loop(0, slots, pull, y_ref[...].astype(F32))
    v = jnp.where(mask, left, 0.0).astype(BF)
    half = v.shape[1] // 2
    x = jnp.concatenate(
        [dot(v, inv_ref[:, :half], 1, 0), dot(v[:, half:], inv_ref[half:, half:], 1, 0)], axis=1
    )
    x = jnp.where(mask, x, 0.0).astype(BF)
    out_ref[0] = x
    x_ref[...] = jnp.where(node_level() == height, x, x_old[...])


def tiles_kernel(sc_ref, above_ref, pick_ref, tile_ref):
    slots, tile_len, _ = pick_ref.shape


    @pl.loop(0, slots)
    def _(s):
        here = pl.ds(pl.multiple_of(s * tile_len, 128), tile_len)
        tile_ref[:, here] = dot(above_ref[s], pick_ref[s], 1, 1).astype(BF)


def own_tiles_kernel(sc_ref, above_ref, map_ref, tile_ref):
    slots, tile_len, _ = map_ref.shape
    rows = above_ref.shape[2]

    @pl.loop(0, slots)
    def _(s):
        here = pl.ds(pl.multiple_of(s * tile_len, 128), tile_len)
        wanted = map_ref[s]
        above = above_ref[s]
        total = jnp.zeros((above.shape[0], tile_len), F32)
        for j in range(rows // 256):
            pick = jnp.concatenate([one_pick(wanted, 2 * j), one_pick(wanted, 2 * j + 1)], axis=1)
            total = total + dot(above[:, j * 256 : (j + 1) * 256], pick, 1, 1)
        tile_ref[:, here] = total.astype(BF)


def place(col, half, upd, inv_ref, upd_ref, blocks):
    count, low = half.shape
    tiles, spare = low // 128, (inv_ref.shape[1] - low) // 128
    base = col * count
    other = (blocks - 1 - col) * count

    @pl.loop(0, count // 16)
    def _(i):
        at = pl.ds(pl.multiple_of(i * 16, 16), 16)
        here = pl.ds(pl.multiple_of(base + i * 16, 16), 16)
        there = pl.ds(pl.multiple_of(other + i * 16, 16), 16)
        for s in range(upd_ref.shape[0]):
            upd_ref[s, here, :] = upd[s, at, :]

        @pl.when(col >= tiles)
        def _():
            inv_ref[here, :low] = half[at, :]

        @pl.when(col < tiles)
        def _():
            for k in range(tiles):
                tile = half[at, k * 128 : (k + 1) * 128].astype(F32)
                own = jnp.full(tile.shape, jnp.where(col >= k, 1, 0), jnp.int32) == 1
                inv_ref[here, k * 128 : (k + 1) * 128] = jnp.where(own, tile, 0.0).astype(BF)
                m = tiles - 1 - k
                if m < spare:
                    to = low + m * 128
                    inv_ref[there, to : to + 128] = jnp.where(own, 0.0, tile).astype(BF)
            inv_ref[here, low:] = jnp.zeros((16, spare * 128), BF)


def gather_kernel(blocks, origins, sc_ref, *refs):
    count = len(origins)
    halves, upds, (inv_ref, upd_ref) = refs[:count], refs[count : 2 * count], refs[-2:]
    for half, upd, (shift, flip) in zip(halves, upds, origins):
        col = lax.rem(col_id() + 2 * shift + blocks, blocks)
        if flip:
            col = col + 1 - 2 * lax.rem(col, 2)
        place(col, half, upd, inv_ref, upd_ref, blocks)


def live_kernel(sc_ref, r_ref, out_ref):
    alive = lax.broadcasted_iota(jnp.int32, r_ref.shape, 0) < live_leaf(sc_ref)
    out_ref[...] = jnp.where(alive, r_ref[...].astype(F32), 0.0).astype(BF)


def prep_kernel(
    sc_ref,
    r_ref,
    fold_ref,
    sides_hbm,
    up_inv_hbm,
    inv_hbm,
    upd_hbm,
    half_ref,
    y_ref,
    keep_ref,
    send_ref,
    base_ref,
    up_inv_ref,
    inv_ref,
    upd_ref,
    sems,
):
    moves = [
        pltpu.make_async_copy(src, dst, sems.at[k])
        for k, (src, dst) in enumerate(
            (
                (up_inv_hbm.at[0], up_inv_ref),
                (inv_hbm.at[0], inv_ref),
                (upd_hbm.at[0], upd_ref),
                (sides_hbm.at[0, 1], base_ref),
            )
        )
    ]
    for move in moves:
        move.start()
    moves[0].wait()
    col = col_id()
    low = half_ref.shape[1]
    tiles, spare = low // 128, fold_ref.shape[1] // 128
    for k in range(tiles):
        mine = up_inv_ref[:, k * 128 : (k + 1) * 128]
        m = tiles - 1 - k
        if m < spare:
            other = fold_ref[:, m * 128 : (m + 1) * 128]
        else:
            other = jnp.zeros_like(mine)
        own = jnp.where((col >= tiles) | (col >= k), 1, 0)
        keep = jnp.full(mine.shape, own, jnp.int32) == 1
        tile = jnp.where(keep, mine.astype(F32), other.astype(F32)).astype(BF)
        half_ref[:, k * 128 : (k + 1) * 128] = tile
    rows_dev = inv_ref.shape[0]
    groups, part, _ = keep_ref.shape
    mask = lax.broadcasted_iota(jnp.int32, y_ref.shape, 0) + col * rows_dev < live_leaf(sc_ref)
    moves[1].wait()
    y = jnp.where(mask, dot(inv_ref[...], r_ref[...], 1, 0), 0.0)
    y_ref[...] = y.astype(BF)
    turned = y.T.astype(BF)
    core = lax.rem(col, 2)
    slots, size = upd_ref.shape[0], upd_ref.shape[2]
    first = jnp.full((part, size), core, jnp.int32) == 0
    moves[2].wait()
    for s in range(slots):
        term = dot(turned, upd_ref[s], 1, 0)
        for g in range(groups):
            a = term[2 * g * part : (2 * g + 1) * part]
            b = term[(2 * g + 1) * part : (2 * g + 2) * part]
            keep_ref[g, :, s * size : (s + 1) * size] = jnp.where(first, a, b).astype(BF)
            send_ref[g, :, s * size : (s + 1) * size] = jnp.where(first, b, a).astype(BF)
    moves[3].wait()
    base = base_ref[...].astype(F32)
    base = jnp.concatenate([base, jnp.zeros((128 - rows_dev, base.shape[1]), F32)], axis=0).T
    first = jnp.full((part, 128), core, jnp.int32) == 0
    for g in range(groups):
        a = base[2 * g * part : (2 * g + 1) * part]
        b = base[(2 * g + 1) * part : (2 * g + 2) * part]
        keep_ref[g, :, slots * size :] = jnp.where(first, a, b).astype(BF)
        send_ref[g, :, slots * size :] = jnp.where(first, b, a).astype(BF)


def join_terms_kernel(sc_ref, keep_ref, got_ref, out_ref):
    groups, part, wide = keep_ref.shape
    size = wide - 128
    first = jnp.full((part, 128), lax.rem(col_id(), 2), jnp.int32) == 0
    for g in range(groups):
        both = keep_ref[g, :, :size].astype(F32) + got_ref[g, :, :size].astype(F32)
        out_ref[g, :, :size] = both.astype(BF)
        own, other = keep_ref[g, :, size:].astype(F32), got_ref[g, :, size:].astype(F32)
        out_ref[g, :, size : size + 128] = jnp.where(first, own, other).astype(BF)
        out_ref[g, :, size + 128 :] = jnp.where(first, other, own).astype(BF)


def leaf_bwd_kernel(sc_ref, tile_ref, y_ref, upd_ref, inv_ref, x_ref, keep_ref, send_ref):
    rows_dev, width = y_ref.shape
    groups, part = keep_ref.shape[0], x_ref.shape[0]
    slots, size = upd_ref.shape[0], upd_ref.shape[2]
    left = y_ref[...].astype(F32)
    for s in range(slots):
        left = left - dot(upd_ref[s], tile_ref[:, s * size : (s + 1) * size], 1, 1)
    mask = lax.broadcasted_iota(jnp.int32, left.shape, 0) + col_id() * rows_dev < live_leaf(sc_ref)
    v = jnp.where(mask, left, 0.0).astype(BF)
    term = dot(inv_ref[...], v, 0, 0)
    core = lax.rem(col_id(), 2)
    first = jnp.full((rows_dev, width), core, jnp.int32) == 0
    first_x = jnp.full((16, 128), core, jnp.int32) == 0
    x = x_ref[...].astype(F32)

    def block(at):
        piece = x[:, at * rows_dev : (at + 1) * rows_dev]
        piece = jnp.concatenate([piece, jnp.zeros((part, 128 - rows_dev), F32)], axis=1)
        return jnp.concatenate([piece, jnp.zeros((16 - part, 128), F32)], axis=0)

    for g in range(groups):
        a = term[2 * g * rows_dev : (2 * g + 1) * rows_dev]
        b = term[(2 * g + 1) * rows_dev : (2 * g + 2) * rows_dev]
        keep_ref[g, :rows_dev] = jnp.where(first, a, b).astype(BF)
        send_ref[g, :rows_dev] = jnp.where(first, b, a).astype(BF)
        xa, xb = block(2 * g), block(2 * g + 1)
        keep_ref[g, rows_dev:] = jnp.where(first_x, xa, xb).astype(BF)
        send_ref[g, rows_dev:] = jnp.where(first_x, xb, xa).astype(BF)


def merge_kernel(sc_ref, keep_ref, got_ref, out_ref):
    rows_dev = keep_ref.shape[1] - 16
    first = jnp.full((16, 128), lax.rem(col_id(), 2), jnp.int32) == 0
    for g in range(keep_ref.shape[0]):
        both = keep_ref[g, :rows_dev].astype(F32) + got_ref[g, :rows_dev].astype(F32)
        out_ref[g, :rows_dev] = both.astype(BF)
        own, other = keep_ref[g, rows_dev:].astype(F32), got_ref[g, rows_dev:].astype(F32)
        out_ref[g, rows_dev : rows_dev + 16] = jnp.where(first, own, other).astype(BF)
        out_ref[g, rows_dev + 16 :] = jnp.where(first, other, own).astype(BF)


def final_kernel(sc_ref, in_ref, out_ref, wide_ref):
    rows_dev = out_ref.shape[1]
    groups, part = in_ref.shape[0], out_ref.shape[2] // (2 * in_ref.shape[0])
    total = in_ref[0, :rows_dev].astype(F32)
    for g in range(1, groups):
        total = total + in_ref[g, :rows_dev].astype(F32)
    mask = lax.broadcasted_iota(jnp.int32, total.shape, 0) + col_id() * rows_dev < live_leaf(sc_ref)
    out_ref[0] = jnp.where(mask, total, 0.0).astype(BF)
    for g in range(groups):
        for p in range(2):
            at, to = rows_dev + 16 * p, (2 * g + p) * part
            wide_ref[to : to + part] = in_ref[g, at : at + 16].astype(F32)[:part]
    out_ref[1] = wide_ref[...].T[:rows_dev].astype(BF)


def shards(
    right_sides, leaf_inverse, upper_inverse, leaf_update, upper_update, live_rows, tile_map
):
    leaf_count = lax.axis_size("leaf")
    col_count = lax.axis_size("col")
    depth = leaf_count.bit_length() - 1
    rows_dev = leaf_inverse.shape[1]
    rows = leaf_inverse.shape[2]
    width = right_sides.shape[3]
    part = width // col_count
    tile_len = tile_map.shape[3]
    leaf_id = lax.axis_index("leaf")

    live_rows = jnp.minimum(live_rows, leaf_inverse.shape[2])
    wide_map = jnp.broadcast_to(tile_map[0, :, :, :, None], (2, depth, tile_len, 128))
    shape = jax.ShapeDtypeStruct
    blocks = col_count
    groups = blocks // 2
    low = rows // 2 + 128
    pairs = [(i, i ^ 1) for i in range(blocks)]
    members = [list(range(p, blocks, 2)) for p in range(2)]

    def along(x, step):
        return lax.ppermute(x, "col", [(i, (i + 2 * step) % blocks) for i in range(blocks)])

    def partner(x):
        return lax.ppermute(x, "col", pairs)

    fold = lax.ppermute(
        upper_inverse[0, :, low:],
        "col",
        [(i, blocks - 1 - i) for i in range(blocks // 2, blocks)],
    )
    r_leaf = lax.all_gather(right_sides[0, 0], "col", axis=0, tiled=True)
    r_leaf = call(live_kernel, shape(r_leaf.shape, BF), live_rows, r_leaf)
    fold, r_leaf = lax.optimization_barrier((fold, r_leaf))
    hbm = pl.BlockSpec(memory_space=pltpu.HBM)
    half, y_leaf, keep, send = call(
        prep_kernel,
        [shape((rows_dev, low), BF), shape((rows_dev, width), BF)]
        + [shape((groups, part, depth * tile_len + 128), BF)] * 2,
        live_rows,
        r_leaf,
        fold,
        right_sides,
        upper_inverse,
        leaf_inverse,
        leaf_update,
        limit=PREP_LIMIT,
        specs=[None, None] + [hbm] * 4,
        scratch=[
            pltpu.VMEM((rows_dev, width), BF),
            pltpu.VMEM((rows_dev, rows), BF),
            pltpu.VMEM((rows_dev, rows), BF),
            pltpu.VMEM((depth, rows_dev, tile_len), BF),
            pltpu.SemaphoreType.DMA((4,)),
        ],
    )
    got = partner(send)
    terms = call(
        join_terms_kernel, shape((groups, part, depth * tile_len + 256), BF), live_rows, keep, got
    )
    swapped = lax.all_to_all(terms, "col", 0, 0, axis_index_groups=members)
    own_upd = upper_update[0, : depth - 1]
    half_a = half_b = half
    upd_a = upd_b = own_upd
    halves, upds, origins = [half, partner(half)], [own_upd, partner(own_upd)], [(0, 0), (0, 1)]
    far = groups // 2
    for hop in range(1, far):
        upd_a, upd_b = along(upd_a, 1), along(upd_b, -1)
        half_a, half_b = along(half_a, 1), along(half_b, -1)
        halves += [half_a, half_b, partner(half_a), partner(half_b)]
        upds += [upd_a, upd_b, partner(upd_a), partner(upd_b)]
        origins += [(-hop, 0), (hop, 0), (-hop, 1), (hop, 1)]
    upd_far = along(upd_b, -1)
    half_far = along(half_a, 1)
    last = [half_far, partner(half_far), upd_far, partner(upd_far)]
    last_origins = [(far, 0), (far, 1)]
    acc, base_up = call(
        leaf_up_kernel,
        [shape((depth + 1, part, rows), BF), shape((part, rows), BF)],
        live_rows,
        swapped,
        wide_map[0],
        tile_map[0, 0],
        scratch=[pltpu.VMEM((depth, part, tile_len), F32)],
    )
    from_leaf = lax.ppermute(acc, "leaf", [(i, i + 1) for i in range(0, leaf_count, 2)])
    pick_up = make_picks(wide_map[1, : depth - 1], rows)
    gathered = [shape((rows, rows), BF), shape((depth - 1, rows, tile_len), BF)]
    inv_up, upd_up = call(
        functools.partial(gather_kernel, blocks, origins), gathered, live_rows, *halves, *upds
    )
    inv_up, upd_up = pl.pallas_call(
        functools.partial(gather_kernel, blocks, last_origins),
        out_shape=gathered,
        in_specs=[SMEM_SPEC] + [VMEM_SPEC] * 6,
        out_specs=[VMEM_SPEC] * 2,
        input_output_aliases={5: 0, 6: 1},
        compiler_params=pltpu.CompilerParams(vmem_limit_bytes=10 << 20),
        name="gather_far",
    )(live_rows, *last, inv_up, upd_up)


    nodes = range(1, leaf_count)

    def level_of(node):
        return (node & -node).bit_length()

    y_up = jnp.zeros((part, rows), BF)
    for height in range(1, depth + 1):
        if height == 1:
            acc_a = acc
            acc_b = from_leaf
        else:
            step = 2 ** (height - 2)
            ups = [i for i in nodes if level_of(i) == height]
            acc_a = lax.ppermute(acc, "leaf", [(i - step, i) for i in ups])
            acc_b = lax.ppermute(acc, "leaf", [(i + step, i) for i in ups])
        if height == 2:
            acc_a, acc_b, next_pick = lax.optimization_barrier((acc_a, acc_b, next_pick))
        outs = [shape((part, rows), BF)]
        if height < depth:
            outs.append(shape((depth - height, part, rows), BF))
        y_up, *rest = call(
            functools.partial(up_kernel, height),
            outs,
            live_rows,
            base_up,
            acc_a,
            acc_b,
            y_up,
            inv_up,
            upd_up,
            pick_up,
        )
        if rest:
            acc = rest[0]
        if height == 1:
            acc, carried = lax.optimization_barrier((acc, from_leaf[depth, :, :tile_len]))
            carried = carried.astype(F32)
            next_map = (carried[:depth] * 128 + carried[depth:]).astype(jnp.int32)
            wide_next = jnp.broadcast_to(next_map[:, :, None], (depth, tile_len, 128))
            next_pick = make_picks(wide_next, rows)

    x_up = jnp.zeros((part, rows), BF)
    abo_a = abo_b = jnp.zeros((1, part, rows), BF)
    for height in range(depth, 0, -1):
        x_up, above = call(
            functools.partial(down_kernel, height),
            [shape((part, rows), BF), shape((depth - height + 1, part, rows), BF)],
            live_rows,
            y_up,
            abo_a,
            abo_b,
            x_up,
            inv_up,
            upd_up,
            pick_up,
        )
        if height == 1:
            sent = call(
                tiles_kernel, shape((part, depth * tile_len), BF), live_rows, above, next_pick
            )
            got = lax.ppermute(sent, "leaf", [(i + 1, i) for i in range(0, leaf_count, 2)])
        else:
            step = 2 ** (height - 2)
            ups = [i for i in nodes if level_of(i) == height]
            abo_a = lax.ppermute(above, "leaf", [(i, i - step) for i in ups])
            abo_b = lax.ppermute(above, "leaf", [(i, i + step) for i in ups])

    tiles = call(
        own_tiles_kernel, shape((part, depth * tile_len), BF), live_rows, above, wide_map[0]
    )
    tiles = jnp.where(leaf_id % 2 == 1, tiles, got)
    tiles = lax.all_gather(tiles, "col", axis=0, tiled=True)
    keep, send = call(
        leaf_bwd_kernel,
        [shape((groups, rows_dev + 16, width), BF)] * 2,
        live_rows,
        tiles,
        y_leaf,
        leaf_update[0],
        leaf_inverse[0],
        x_up,
    )
    merged = call(
        merge_kernel, shape((groups, rows_dev + 32, width), BF), live_rows, keep, partner(send)
    )
    swapped = lax.all_to_all(merged, "col", 0, 0, axis_index_groups=members)
    return call(
        final_kernel,
        shape((2, rows_dev, width), BF),
        live_rows,
        swapped,
        scratch=[pltpu.VMEM((width, 128), F32)],
    )[None]


def solution(mesh):
    placed = (
        P("leaf", None, "col", None),
        P("leaf", "col", None),
        P("leaf", "col", None),
        P("leaf", None, "col", None),
        P("leaf", None, "col", None),
        P("leaf", None),
        P("leaf", None, None, None),
    )

    return jax.shard_map(
        shards, mesh=mesh, in_specs=placed, out_specs=P("leaf", None, "col", None), check_vma=False
    )
```
